32 devices in a mesh: feeder: 8 (over z, core), tm: 4 (over y, x).
Axes of the slice: x: 2, y: 2, z: 4, core: 2. Of those that a mesh axis runs over, the one named last changes fastest.
Arguments:
- node_load: bfloat16 [128, 64, 24, 512], P('feeder', None, 'tm'), may hold values from -6 to 6
- drive_map: bfloat16 [128, 512, 256], P('feeder'), may hold values from -0.25 to 0.25
- decay_rate: float32 [128, 24, 256], P('feeder', 'tm'), may hold values from 0.45 to 1
- counts: int32 [128], P('feeder'), may hold values from 64 to 256
- out_map: float32 [128, 2, 256], P('feeder'), may hold values from -0.375 to 0.375
- area_of: int32 [128, 1], replicated, may hold values from 0 to 7; in each aligned block of 16 rows (0 to 15, 16 to 31, ...) at most 2 rows name the same one
- head_bus: int32 [128], replicated, may hold values from 0 to 255
- rule_of: int32 [128], replicated, may hold values from 0 to 15
- rule_knots: int32 [16, 8], replicated, may hold values from -3200 to 2400, as said below
- levels: int32 [16, 8], replicated, may hold values from -1000 to 1000
- sensitivity: float32 [8, 2, 256, 256], P('feeder'), may hold values from -0.6 to 0.6
Outputs:
- setpoints: float32 [128, 24, 64], P('feeder', 'tm')
The draws below stay inside these ranges and needn't reach their ends.
Inputs may be any that keep to these rules, and one draw needn't show every extreme that they name: `area_of`: in each aligned block of 16 feeders no area is named by more than 2 feeders, a bound that some block reaches. `rule_knots`: each row strictly increasing, neighbouring breakpoints 200 to 800 apart.
All inputs are finite; a program needn't handle non-finite values.
Results may differ from the reference program's by a relative error of at most 0.00045.
Values sent between devices are 32-bit elements; how exact they have to be, the bound alone decides.
A program may use at most 64 MiB of HBM per device.

```python
import math
import jax
import jax.numpy as jnp
import numpy as np
from jax import lax

NODE = 512
STATE = 256
BUS = 256
CAP = 2
RULES = 16
KNOTS = 8
FEED_DEV = 16
SCEN = 64
LATERAL_COUNT = 128
AREAS = 8
HORIZON_TICKS = 24


def draw_decay_rate(key, part):
    speed_seed, surge_seed, multiplier_seed = jax.random.split(jax.random.fold_in(key, 11), 3)
    lowest = math.log(0.3 / HORIZON_TICKS)
    highest = math.log(1.0 / 30.0)
    spread = jax.random.uniform(speed_seed, (LATERAL_COUNT, 1, STATE), jnp.float32)
    rates = jnp.exp(lowest + (highest - lowest) * spread)
    nominal_magnitude = jnp.exp(-rates)
    surge_size = jax.random.uniform(surge_seed, (LATERAL_COUNT, HORIZON_TICKS, 1), jnp.float32) < 3.0 / HORIZON_TICKS
    multiplier_number = jax.random.uniform(multiplier_seed, (LATERAL_COUNT, HORIZON_TICKS, 1), jnp.float32, 0.5, 0.8)
    return (nominal_magnitude * jnp.where(surge_size, multiplier_number, 1.0)).astype(jnp.float32)


def draw_rule_knots(key, part):
    spacing = jax.random.randint(jax.random.fold_in(key, 23), (RULES, KNOTS), 200, 801).astype(jnp.int32)
    totals = jnp.cumsum(spacing, axis=1).astype(jnp.int32)
    middle = KNOTS // 2
    return (totals - totals[:, middle:middle + 1]).astype(jnp.int32)


def touch_ends(array, rng, smallest, high):
    place = [jax.random.randint(jax.random.fold_in(rng, axis), (), 0, length) for axis, length in enumerate(array.shape)]
    main_axis = array.shape.index(max(array.shape))
    next_to = place[:main_axis] + [(place[main_axis] + 1) % array.shape[main_axis]] + place[main_axis + 1:]
    return array.at[tuple(place)].set(smallest).at[tuple(next_to)].set(high)


def block_levels(rng, dims, cuts, smallest, largest):
    factor_of = 1.0
    for position, parts in cuts:
        heights = jax.random.uniform(jax.random.fold_in(jax.random.fold_in(rng, 6), position), (parts,), jnp.float32, smallest / len(cuts), largest / len(cuts))
        factor_of = factor_of * jnp.repeat(jnp.exp(heights), dims[position] // parts).reshape((-1,) + (1,) * (len(dims) - 1 - position))
    return factor_of


def shared_out(stream_key, own, number, rows, amount, top, bound, skew):
    sequence = jax.random.permutation(stream_key, amount)
    packed, ordinary = shares(amount, rows * top, bound, skew, True), shares(amount, rows * top, bound, skew, False)
    places = jnp.arange(amount)

    def named(lengths, turn):
        used = int((lengths > 0).sum())
        fixed = max(1, used // 4)
        moved = fixed + (places - fixed + turn * (used - fixed)) % max(1, amount - fixed)
        return jnp.zeros((amount,), jnp.int32).at[sequence[jnp.where(places < fixed, places, moved)]].set(jnp.asarray(lengths, jnp.int32))

    lengths = jnp.where(number % 4 == 0, named(packed, number // 4), named(ordinary, number - number // 4 - 1))
    mixed = jax.random.permutation(jax.random.fold_in(own, 3), amount)
    donor, sink = mixed[0:amount // 2 * 2:2], mixed[1:amount // 2 * 2:2]
    room = jnp.minimum(lengths[donor] - 1, bound - lengths[sink]) // 2
    room = jnp.where((donor == sequence[0]) | (sink == sequence[0]) | (lengths[sink] == 0), 0, jnp.maximum(room, 0))
    moved = jax.random.randint(jax.random.fold_in(own, 4), (amount // 2,), 0, 1 << 20) % (room + 1)
    lengths = lengths.at[donor].add(-moved).at[sink].add(moved)
    items = jnp.searchsorted(jnp.cumsum(lengths), jnp.arange(rows * top), side="right").astype(jnp.int32)
    grid = items.reshape(top, rows).T
    grid = grid[jax.random.permutation(jax.random.fold_in(own, 1), rows)]
    turn = jax.random.randint(jax.random.fold_in(own, 2), (rows, 1), 0, top)
    return jnp.take_along_axis(grid, (jnp.arange(top)[None, :] + turn) % top, axis=1)


def shares(amount, total, reach, skew, full):
    weights = [(1 << 20) // math.isqrt(standing ** skew) + 1 for standing in range(1, amount + 1)]
    largest = reach if full else min(reach, max(-(-total // amount), total * weights[0] // sum(weights)))
    least = 1 if total - largest >= amount - 1 else 0
    given, rest = [largest] + [least] * (amount - 1), total - largest - least * (amount - 1)
    while rest > 0:
        movable = [i for i in range(1, amount) if given[i] < largest] or [i for i in range(1, amount) if given[i] < reach]
        whole, left = sum([weights[i] for i in movable]), rest
        for i in movable:
            addition = min(reach - given[i], max(1, left * weights[i] // whole), rest)
            given[i] = given[i] + addition
            rest = rest - addition
    return np.array(given)


def gaussian(rng, dims, scale, limit, cuts=(), kind=jnp.bfloat16):
    level = block_levels(rng, dims, cuts, -0.22, 0.18) if cuts else 1.0
    array = jax.random.normal(rng, dims, jnp.float32) * scale * level
    return jnp.minimum(jnp.maximum(array, -limit), limit).astype(kind)


def setup_inputs(seed: int = 0) -> dict:
    keys = jax.random.split(jax.random.key(seed), 12)
    node_load = gaussian(keys[0], (LATERAL_COUNT, SCEN, HORIZON_TICKS, NODE), 1.0, 6.0, ((0, 8), (2, 4)))
    drive_map = gaussian(keys[1], (LATERAL_COUNT, NODE, STATE), NODE ** -0.5, 0.25, ((0, 8),))
    decay_rate = draw_decay_rate(jax.random.fold_in(keys[11], 71), 0)
    counts = touch_ends(jax.random.randint(keys[3], (LATERAL_COUNT,), STATE // 4, STATE + 1), jax.random.fold_in(keys[3], 1), STATE // 4, STATE).astype(jnp.int32)
    out_map = gaussian(keys[4], (LATERAL_COUNT, 2, STATE), STATE ** -0.5, 0.375, ((0, 8),), jnp.float32)
    area_of_keys = jax.random.split(jax.random.fold_in(keys[5], 1), LATERAL_COUNT // FEED_DEV)
    area_of_turns = jax.random.permutation(jax.random.fold_in(keys[5], 3), LATERAL_COUNT // FEED_DEV)
    area_of = jax.vmap(lambda own, number: shared_out(jax.random.fold_in(keys[5], 2), own, number, FEED_DEV, AREAS, 1, CAP, 2))(area_of_keys, area_of_turns).reshape((LATERAL_COUNT, 1))
    head_bus = touch_ends(jax.random.randint(keys[6], (LATERAL_COUNT,), 0, BUS), jax.random.fold_in(keys[6], 1), 0, BUS - 1).astype(jnp.int32)
    rule_of = touch_ends(jax.random.randint(keys[7], (LATERAL_COUNT,), 0, RULES), jax.random.fold_in(keys[7], 1), 0, RULES - 1).astype(jnp.int32)
    rule_knots = draw_rule_knots(jax.random.fold_in(keys[11], 71), 0)
    levels = touch_ends(jax.random.randint(keys[9], (RULES, KNOTS), -1000, 1001), jax.random.fold_in(keys[9], 1), -1000, 1000).astype(jnp.int32)
    sensitivity = gaussian(keys[10], (AREAS, 2, BUS, BUS), 0.1, 0.6, ((0, 8),), jnp.float32)
    return dict(node_load=node_load, drive_map=drive_map, decay_rate=decay_rate, counts=counts, out_map=out_map, area_of=area_of, head_bus=head_bus, rule_of=rule_of, rule_knots=rule_knots, levels=levels, sensitivity=sensitivity)


def setpoint_rule(volts, knot_volts, knot_levels):
    result = knot_levels[:, 0:1] + jnp.zeros_like(volts)
    for piece in range(knot_volts.shape[1] - 1):
        span_width = knot_volts[:, piece + 1:piece + 2] - knot_volts[:, piece:piece + 1]
        slope = (knot_levels[:, piece + 1:piece + 2] - knot_levels[:, piece:piece + 1]) / span_width
        result = result + slope * jnp.clip(volts - knot_volts[:, piece:piece + 1], 0.0, span_width)
    return result


def reference(node_load, drive_map, decay_rate, counts, out_map, area_of, head_bus, rule_of, rule_knots, levels, sensitivity):
    state_ids = jnp.arange(STATE, dtype=jnp.int32)

    def feeder_run(inputs):
        loads, mapping, retain, live_count, output_mapping = inputs
        live = (state_ids < live_count).astype(jnp.float32)
        drive = jnp.einsum('ctn,ns->cts', loads.astype(jnp.float32), mapping.astype(jnp.float32), precision=lax.Precision.HIGHEST) * live

        def advance(current, pair):
            keep, push = pair
            current = keep[None, :] * current + push
            return current, current

        _, history_record = lax.scan(advance, jnp.zeros((SCEN, STATE), jnp.float32), (retain, jnp.swapaxes(drive, 0, 1)))
        flow_value = jnp.einsum('dqp,up->udq', history_record, output_mapping, precision=lax.Precision.HIGHEST)
        return flow_value.reshape(2, HORIZON_TICKS * SCEN)

    head_flow = lax.map(feeder_run, (node_load, drive_map, decay_rate, counts, out_map))
    area_ids = area_of[:, 0]
    bus_hot = (head_bus[:, None] == jnp.arange(BUS, dtype=jnp.int32)[None, :]).astype(jnp.float32)

    def area_run(inputs):
        area_index, sens_block = inputs
        chosen = bus_hot * (area_ids == area_index).astype(jnp.float32)[:, None]
        bus_flow = jnp.einsum('fb,fkr->kbr', chosen, head_flow, precision=lax.Precision.HIGHEST)
        return jnp.einsum('kbe,ker->br', sens_block, bus_flow, precision=lax.Precision.HIGHEST)

    volt_shift = lax.map(area_run, (jnp.arange(AREAS, dtype=jnp.int32), sensitivity))
    volts = volt_shift[area_ids, head_bus]
    knot_volts = rule_knots.astype(jnp.float32)[rule_of] / 1000.0
    knot_levels = levels.astype(jnp.float32)[rule_of] / 1000.0
    settings = setpoint_rule(volts, knot_volts, knot_levels)
    return settings.reshape(LATERAL_COUNT, HORIZON_TICKS, SCEN)
```

```python
import functools

import jax
import jax.numpy as jnp
from jax import lax
from jax.experimental import pallas as pl
from jax.experimental.pallas import tpu as pltpu
from jax.sharding import PartitionSpec as P

HIGH = lax.Precision.HIGHEST
NT = (((1,), (1,)), ((), ()))
MESH = pl.DeviceIdType.MESH
CAP = 2
SLOT_ROWS = 8
BATCHES = 4


def split(value):
    upper = value.astype(jnp.bfloat16)
    return upper, (value - upper.astype(jnp.float32)).astype(jnp.bfloat16)


def dot(left, right):
    return jnp.dot(left, right, preferred_element_type=jnp.float32)


def dot_nt(left, right):
    return lax.dot_general(left, right, NT, preferred_element_type=jnp.float32)


def one_hot(condition):
    return jnp.where(condition, 1.0, 0.0).astype(jnp.bfloat16)


def kernel(
    groups,
    turns,
    load_hbm,
    map_hbm,
    decay_hbm,
    counts_hbm,
    out_map_hbm,
    area_hbm,
    bus_hbm,
    rule_hbm,
    knots_hbm,
    levels_hbm,
    sens_hbm,
    out_ref,
    load_ref,
    map_ref,
    sens_ref,
    decay_ref,
    counts_ref,
    out_map_ref,
    area_ref,
    bus_ref,
    rule_ref,
    knots_ref,
    levels_ref,
    later_decay,
    pair_send,
    pair_recv,
    weight_ref,
    upper_ref,
    lower_ref,
    column_ref,
    local_ref,
    rank_ref,
    rule_vals,
    flow_send,
    flow_recv,
    volt_send,
    volt_recv,
    load_sems,
    small_sems,
    decay_sems,
    pair_sems,
    flow_sems,
    volt_sems,
):
    group, turn = lax.axis_index("feeder"), lax.axis_index("tm")
    per_dev, span, scen, nodes = load_ref.shape
    width = map_ref.shape[2]
    half = per_dev // 2
    couples = span // 2
    feeders = bus_ref.shape[1]
    buses = sens_ref.shape[1]
    rows = weight_ref.shape[1] // per_dev
    later_rows = rows // 2
    piece = couples * 2 * half
    batch = per_dev // BATCHES

    barrier = pltpu.get_barrier_semaphore()
    for step in range(1, turns):
        pl.semaphore_signal(
            barrier,
            inc=1,
            device_id=(group, lax.rem(turn + step, turns)),
            device_id_type=MESH,
        )
    for step in range(1, groups):
        pl.semaphore_signal(
            barrier,
            inc=1,
            device_id=(lax.rem(group + step, groups), turn),
            device_id_type=MESH,
        )

    small = [
        pltpu.make_async_copy(source, target, small_sems.at[i])
        for i, (source, target) in enumerate(
            [
                (area_hbm, area_ref),
                (bus_hbm, bus_ref),
                (sens_hbm.at[0], sens_ref),
                (counts_hbm, counts_ref),
                (out_map_hbm, out_map_ref),
                (decay_hbm, decay_ref),
                (rule_hbm, rule_ref),
                (knots_hbm, knots_ref),
                (levels_hbm, levels_ref),
            ]
        )
    ]
    for copy in small:
        copy.start()

    def load_copies(b):
        own = pl.ds(b * batch, batch)
        return (
            pltpu.make_async_copy(map_hbm.at[own], map_ref.at[own], load_sems.at[0, b]),
            pltpu.make_async_copy(load_hbm.at[own], load_ref.at[own], load_sems.at[1, b]),
        )

    for b in range(BATCHES):
        for copy in load_copies(b):
            copy.start()

    with jax.named_scope("prep_ranks"):
        small[0].wait()
        small[1].wait()
        ids_row = lax.broadcasted_iota(jnp.int32, (feeders, feeders), 1)
        ids_col = lax.broadcasted_iota(jnp.int32, (feeders, feeders), 0)
        area_row = area_ref[...].astype(jnp.float32)
        area_col = jnp.concatenate([area_row] * 8, axis=0).T[:, :1]
        peers = (area_col == area_row) & (ids_col // per_dev == ids_row // per_dev)
        rank_row = jnp.sum(jnp.where(peers & (ids_col < ids_row), 1.0, 0.0), axis=0, keepdims=True)
        rank_ref[...] = jnp.concatenate([area_row] * 4 + [rank_row] * 4, axis=0).T

        place = lax.broadcasted_iota(jnp.int32, (groups * SLOT_ROWS, feeders), 0)
        owner = lax.broadcasted_iota(jnp.int32, (groups * SLOT_ROWS, feeders), 1) // per_dev
        slot = lax.rem(place, SLOT_ROWS)
        wanted = (place // SLOT_ROWS == owner) & (area_ref[...] == group) & (slot < 2 * CAP)
        chosen = one_hot(wanted & (rank_row == lax.rem(slot, CAP).astype(jnp.float32)))
        bus_ids = lax.broadcasted_iota(jnp.int32, (buses, feeders), 0)
        owned = (bus_ids == bus_ref[...]) & (area_ref[...] == group)
        hot = one_hot(owned)
        sources = dot_nt(chosen, hot).astype(jnp.bfloat16)

    with jax.named_scope("prep_pairs"):
        small[2].wait()
        picked = [sum(dot_nt(sources, term) for term in split(sens_ref[k])) for k in range(2)]
        kind = lax.broadcasted_iota(jnp.int32, (groups * SLOT_ROWS, buses), 0)
        kind = lax.rem(kind, SLOT_ROWS) // CAP
        picked = jnp.where(kind == 0, picked[0], picked[1])
        pairs = sum(dot(term, hot) for term in split(picked))
        pair_send[...] = pairs.reshape(groups, SLOT_ROWS, feeders)

    def decay_copy(part, step):
        own = pl.ds(part * half, half)
        return pltpu.make_async_remote_copy(
            src_ref=decay_hbm.at[:, own],
            dst_ref=later_decay.at[step - 1, :, own],
            send_sem=decay_sems.at[0, part, step - 1],
            recv_sem=decay_sems.at[1, part, step - 1],
            device_id=(group, turn - step),
            device_id_type=MESH,
        )

    def pair_copy(step):
        target = lax.rem(group + step, groups)
        return pltpu.make_async_remote_copy(
            src_ref=pair_send.at[target],
            dst_ref=pair_recv.at[step],
            send_sem=pair_sems.at[0, step - 1],
            recv_sem=pair_sems.at[1, step - 1],
            device_id=(target, turn),
            device_id_type=MESH,
        )

    with jax.named_scope("barrier"):
        pl.semaphore_wait(barrier, turns + groups - 2)
    for part in range(2):
        for step in range(1, turns):

            @pl.when(turn >= step)
            def _():
                decay_copy(part, step).start()

    for step in range(1, groups):
        pair_copy(step).start()

    with jax.named_scope("prep_columns"):
        small[3].wait()
        small[4].wait()
        small[5].wait()
        same = lax.broadcasted_iota(jnp.int32, (per_dev, per_dev), 0) == lax.broadcasted_iota(
            jnp.int32, (per_dev, per_dev), 1
        )
        limit = jnp.sum(
            jnp.where(same, counts_ref[...].astype(jnp.float32), 0.0), axis=1, keepdims=True
        )
        state_ids = lax.broadcasted_iota(jnp.int32, (per_dev, width), 1).astype(jnp.float32)
        maps = [jnp.where(state_ids < limit, out_map_ref[:, k, :], 0.0) for k in range(2)]
        parts = [split(m) for m in maps]
        columns = [p[0] for p in parts] + [p[1] for p in parts]
        blank = jnp.zeros((128 - 4 * per_dev, width), jnp.float32)
        columns = [c.astype(jnp.float32) for c in columns] + [blank]
        columns = jnp.concatenate(columns, axis=0).T.astype(jnp.bfloat16)
        lane_ids = lax.rem(lax.broadcasted_iota(jnp.int32, (1, 128), 1), per_dev)
        for f in range(per_dev):
            column_ref[f * width : (f + 1) * width] = columns * one_hot(lane_ids == f)

    def states(b):
        for copy in load_copies(b):
            copy.wait()
        for f in range(b * batch, (b + 1) * batch):
            drive = dot(load_ref[f].reshape(span * scen, nodes), map_ref[f])
            state = drive[:scen]
            own = slice(f * width, (f + 1) * width)
            for t in range(span):
                now = slice(t * scen, (t + 1) * scen)
                if t:
                    state = decay_ref[t, f : f + 1, :] * state + drive[now]
                upper_ref[now, own], lower_ref[now, own] = split(state)

    def local_flow(b):
        own = slice(b * batch * width, (b + 1) * batch * width)
        value = dot(upper_ref[:, own], column_ref[own]) + dot(lower_ref[:, own], column_ref[own])
        local_ref[...] = value if b == 0 else local_ref[...] + value

    with jax.named_scope("states0"):
        states(0)

    for b in range(1, BATCHES):
        with jax.named_scope("states%d" % b):
            states(b)
            local_flow(b - 1)

    def put_rows(row, value):
        for lane in range(width // 128):
            weight_ref[lane, pl.ds(row, half, stride=rows), :] = value[
                :, lane * 128 : (lane + 1) * 128
            ]

    def products(part):
        own = slice(part * half, (part + 1) * half)
        product = jnp.ones((half, width), jnp.float32)
        for step in range(turns - 1):
            for t in range(span):
                product = product * later_decay[step, t, own]
                for k in range(2):
                    row = (t % 2) * later_rows + (step * couples + t // 2) * 2 + k
                    put_rows(part * half * rows + row, maps[k][own] * product)

    end = slice((span - 1) * scen, span * scen)

    def later_flow(part):
        for index in range(half):
            f = part * half + index
            weight = jnp.concatenate(
                [weight_ref[lane, f * rows : (f + 1) * rows, :] for lane in range(width // 128)],
                axis=1,
            )
            stacked = jnp.concatenate(split(weight), axis=0)
            own = slice(f * width, (f + 1) * width)
            later = dot_nt(stacked, upper_ref[end, own]) + dot_nt(stacked, lower_ref[end, own])
            later = later[:rows] + later[rows:]
            flow_send[part, pl.ds(index, later_rows, stride=half), :] = jnp.concatenate(
                [later[:later_rows], later[later_rows:]], axis=1
            )

    def flow_copy(part, step):
        return pltpu.make_async_remote_copy(
            src_ref=flow_send.at[part, pl.ds((step - 1) * piece, piece)],
            dst_ref=flow_recv.at[part, step - 1],
            send_sem=flow_sems.at[0, part, step - 1],
            recv_sem=flow_sems.at[1, part, step - 1],
            device_id=(group, turn + step),
            device_id_type=MESH,
        )

    def send_flow(part):
        for step in range(1, turns):

            @pl.when(turn + step < turns)
            def _():
                flow_copy(part, step).start()

    for part in range(2):
        with jax.named_scope("decaywait%d" % part):
            for step in range(1, turns):

                @pl.when(turn >= step)
                def _():
                    decay_copy(part, step).wait_send()

                @pl.when(turn + step < turns)
                def _():
                    decay_copy(part, step).wait_recv()

        if turns > 1:
            with jax.named_scope("later%d" % part):
                products(part)
                later_flow(part)
        send_flow(part)

    with jax.named_scope("local_last"):
        local_flow(BATCHES - 1)
        local = local_ref[...].T
        local = local[: 2 * per_dev] + local[2 * per_dev : 4 * per_dev]

    with jax.named_scope("rules"):
        for copy in small[6:]:
            copy.wait()
        rules = knots_ref.shape[1]
        rule_ids = lax.broadcasted_iota(jnp.int32, (rules, feeders), 0)
        rule_hot = jnp.where(rule_ids == rule_ref[...], 1.0, 0.0)
        table = jnp.concatenate(
            [knots_ref[...].astype(jnp.float32), levels_ref[...].astype(jnp.float32)], axis=0
        )
        chosen = jnp.dot(table, rule_hot, precision=HIGH, preferred_element_type=jnp.float32)
        rule_vals[...] = (chosen / 1000.0).T

    with jax.named_scope("effect"):
        pair_recv[0] = pair_send[group]
        for step in range(1, groups):
            pair_copy(step).wait()
        places = groups * SLOT_ROWS
        mine = rank_ref[pl.ds(pl.multiple_of(group * per_dev, 8), per_dev), :]
        mine = jnp.concatenate([mine, mine], axis=0)
        place = lax.broadcasted_iota(jnp.int32, (2 * per_dev, places), 1)
        kind = lax.broadcasted_iota(jnp.int32, (2 * per_dev, places), 0) // per_dev
        source = lax.rem(group + groups - place // SLOT_ROWS, groups).astype(jnp.float32)
        slot = lax.rem(place, SLOT_ROWS)
        taken = (mine[:, :1] == source) & (slot // CAP == kind)
        taken = one_hot(taken & (mine[:, 4:5] == lax.rem(slot, CAP).astype(jnp.float32)))
        upper, lower = [
            dot(taken, term).T.astype(jnp.bfloat16)
            for term in split(pair_recv[...].reshape(places, feeders))
        ]
        effect = jnp.concatenate([upper, upper, lower], axis=1)

    with jax.named_scope("flowwait"):
        for part in range(2):
            for step in range(1, turns):

                @pl.when(turn >= step)
                def _():
                    flow_copy(part, step).wait_recv()

                @pl.when(turn < step)
                def _():
                    flow_recv[part, step - 1] = jnp.zeros((piece, 2 * scen), jnp.float32)

    def volt_copy(step):
        target = lax.rem(group + step, groups)
        return pltpu.make_async_remote_copy(
            src_ref=volt_send.at[target],
            dst_ref=volt_recv.at[step - 1],
            send_sem=volt_sems.at[0, step - 1],
            recv_sem=volt_sems.at[1, step - 1],
            device_id=(target, turn),
            device_id_type=MESH,
        )

    with jax.named_scope("shift"):
        arrived = [
            sum(flow_recv[part, step] for step in range(turns - 1))
            if turns > 1
            else jnp.zeros((piece, 2 * scen), jnp.float32)
            for part in range(2)
        ]
        for couple in range(couples):
            extra = [
                arrived[part][(couple * 2 + k) * half : (couple * 2 + k + 1) * half]
                for k in range(2)
                for part in range(2)
            ]
            sources = local[:, couple * 2 * scen : (couple + 1) * 2 * scen]
            upper, lower = split(sources + jnp.concatenate(extra, axis=0))
            sources = jnp.concatenate([upper, lower, upper], axis=0)
            volt_send[:, couple] = dot(effect, sources).reshape(groups, per_dev, 2 * scen)

    for step in range(1, groups):
        volt_copy(step).start()

    mine = rule_vals[pl.ds(pl.multiple_of(group * per_dev, 8), per_dev), :]
    knot_count = knots_ref.shape[0]
    knots = [mine[:, i : i + 1] for i in range(knot_count)]
    levels = [mine[:, knot_count + i : knot_count + i + 1] for i in range(knot_count)]
    spans = [knots[i + 1] - knots[i] for i in range(knot_count - 1)]
    slopes = [(levels[i + 1] - levels[i]) / spans[i] for i in range(knot_count - 1)]
    with jax.named_scope("voltwait"):
        volts = volt_send[group]
        for step in range(1, groups):
            volt_copy(step).wait_recv()
            volts = volts + volt_recv[step - 1]
    with jax.named_scope("rule"):
        for couple in range(couples):
            value = volts[couple]
            result = levels[0] + jnp.zeros_like(value)
            for i in range(knot_count - 1):
                inside = jnp.minimum(jnp.maximum(value - knots[i], 0.0), spans[i])
                result = result + slopes[i] * inside
            out_ref[2 * couple] = result[:, :scen]
            out_ref[2 * couple + 1] = result[:, scen:]

    for step in range(1, groups):
        volt_copy(step).wait_send()
    for part in range(2):
        for step in range(1, turns):

            @pl.when(turn + step < turns)
            def _():
                flow_copy(part, step).wait_send()


def per_device(
    node_load,
    drive_map,
    decay_rate,
    counts,
    out_map,
    area_of,
    head_bus,
    rule_of,
    rule_knots,
    levels,
    sensitivity,
):
    groups, turns = lax.axis_size("feeder"), lax.axis_size("tm")
    per_dev, scen, span, nodes = node_load.shape
    width = drive_map.shape[2]
    feeders = head_bus.shape[0]
    buses = sensitivity.shape[2]
    half, couples = per_dev // 2, span // 2
    later_rows = -(-(turns - 1) * span // 8) * 8
    rows = max(2 * later_rows, 8)
    piece = couples * 2 * half
    vmem = pl.BlockSpec(memory_space=pltpu.VMEM)
    hbm = pl.BlockSpec(memory_space=pltpu.HBM)
    f32, i32 = jnp.float32, jnp.int32
    dma = pltpu.SemaphoreType.DMA
    operands = (
        jnp.transpose(node_load, (0, 2, 1, 3)),
        drive_map,
        jnp.transpose(decay_rate, (1, 0, 2)),
        counts.reshape(1, per_dev),
        out_map,
        area_of.reshape(1, feeders),
        head_bus.reshape(1, feeders),
        rule_of.reshape(1, feeders),
        rule_knots.T,
        levels.T,
        sensitivity,
    )
    settings = pl.pallas_call(
        functools.partial(kernel, groups, turns),
        out_shape=jax.ShapeDtypeStruct((span, per_dev, scen), f32),
        in_specs=[hbm] * len(operands),
        out_specs=vmem,
        scratch_shapes=[
            pltpu.VMEM((per_dev, span, scen, nodes), node_load.dtype),
            pltpu.VMEM((per_dev, nodes, width), drive_map.dtype),
            pltpu.VMEM((2, buses, buses), f32),
            pltpu.VMEM((span, per_dev, width), f32),
            pltpu.VMEM((1, per_dev), i32),
            pltpu.VMEM(out_map.shape, f32),
            pltpu.VMEM((1, feeders), i32),
            pltpu.VMEM((1, feeders), i32),
            pltpu.VMEM((1, feeders), i32),
            pltpu.VMEM(rule_knots.shape[::-1], i32),
            pltpu.VMEM(levels.shape[::-1], i32),
            pltpu.VMEM((turns - 1, span, per_dev, width), f32),
            pltpu.VMEM((groups, SLOT_ROWS, feeders), f32),
            pltpu.VMEM((groups, SLOT_ROWS, feeders), f32),
            pltpu.VMEM((width // 128, per_dev * rows, 128), f32),
            pltpu.VMEM((span * scen, per_dev * width), jnp.bfloat16),
            pltpu.VMEM((span * scen, per_dev * width), jnp.bfloat16),
            pltpu.VMEM((per_dev * width, 128), jnp.bfloat16),
            pltpu.VMEM((span * scen, 128), f32),
            pltpu.VMEM((feeders, 8), f32),
            pltpu.VMEM((feeders, 2 * rule_knots.shape[1]), f32),
            pltpu.VMEM((2, later_rows * half, 2 * scen), f32),
            pltpu.VMEM((2, turns - 1, piece, 2 * scen), f32),
            pltpu.VMEM((groups, couples, per_dev, 2 * scen), f32),
            pltpu.VMEM((groups - 1, couples, per_dev, 2 * scen), f32),
            dma((2, BATCHES)),
            dma((9,)),
            dma((2, 2, turns - 1)),
            dma((2, groups - 1)),
            dma((2, 2, turns - 1)),
            dma((2, groups - 1)),
        ],
        compiler_params=pltpu.CompilerParams(
            collective_id=0, has_side_effects=True, vmem_limit_bytes=VMEM_LIMIT
        ),
    )(*[pltpu.with_memory_space_constraint(x, pltpu.HBM) for x in operands])
    return jnp.transpose(settings, (1, 0, 2))


VMEM_LIMIT = 48 * 2**20


def solution(mesh):
    return jax.shard_map(
        per_device,
        mesh=mesh,
        in_specs=(
            P("feeder", None, "tm", None),
            P("feeder", None, None),
            P("feeder", "tm", None),
            P("feeder"),
            P("feeder", None, None),
            P(),
            P(),
            P(),
            P(),
            P(),
            P("feeder", None, None, None),
        ),
        out_specs=P("feeder", "tm", None),
        check_vma=False,
    )
```

```python
import functools

import jax
import jax.numpy as jnp
from jax import lax
from jax.experimental import pallas as pl
from jax.experimental.pallas import tpu as pltpu
from jax.sharding import PartitionSpec as P

HIGH = lax.Precision.HIGHEST
NT = (((1,), (1,)), ((), ()))
MESH = pl.DeviceIdType.MESH
CAP = 2
SLOT_ROWS = 8
BATCHES = 4
NEAR = 2


def split(value):
    upper = value.astype(jnp.bfloat16)
    return upper, (value - upper.astype(jnp.float32)).astype(jnp.bfloat16)


def dot(left, right):
    return jnp.dot(left, right, preferred_element_type=jnp.float32)


def dot_nt(left, right):
    return lax.dot_general(left, right, NT, preferred_element_type=jnp.float32)


def one_hot(condition):
    return jnp.where(condition, 1.0, 0.0).astype(jnp.bfloat16)


def kernel(
    groups,
    turns,
    load_hbm,
    map_hbm,
    decay_hbm,
    counts_hbm,
    out_map_hbm,
    area_hbm,
    bus_hbm,
    rule_hbm,
    knots_hbm,
    levels_hbm,
    sens_hbm,
    out_ref,
    load_ref,
    map_ref,
    sens_ref,
    decay_ref,
    counts_ref,
    out_map_ref,
    area_ref,
    bus_ref,
    rule_ref,
    knots_ref,
    levels_ref,
    later_decay,
    pair_send,
    pair_recv,
    weight_ref,
    state_ref,
    column_ref,
    local_ref,
    rank_ref,
    rule_vals,
    flow_send,
    flow_recv,
    volt_send,
    volt_recv,
    load_sems,
    small_sems,
    reach_sems,
    decay_sems,
    pair_sems,
    flow_sems,
    volt_sems,
):
    group, turn = lax.axis_index("feeder"), lax.axis_index("tm")
    per_dev, span, scen, nodes = load_ref.shape
    width = map_ref.shape[2]
    half = per_dev // 2
    couples = span // 2
    feeders = bus_ref.shape[1]
    buses = sens_ref.shape[1]
    rows = weight_ref.shape[1] // per_dev
    later_rows = rows // 2
    piece = couples * 2 * half
    batch = per_dev // BATCHES

    barrier = pltpu.get_barrier_semaphore()
    for step in range(1, turns):
        pl.semaphore_signal(
            barrier,
            inc=1,
            device_id=(group, lax.rem(turn + step, turns)),
            device_id_type=MESH,
        )

    def tell(semaphore, distance):
        @pl.when(group + distance < groups)
        def _():
            pl.semaphore_signal(
                semaphore, inc=1, device_id=(group + distance, turn), device_id_type=MESH
            )

        @pl.when(group >= distance)
        def _():
            pl.semaphore_signal(
                semaphore, inc=1, device_id=(group - distance, turn), device_id_type=MESH
            )

    def tellers(distance):
        above = lax.div(2 * groups - 1 - group - distance, groups)
        return above + lax.div(groups + group - distance, groups)

    for distance in range(1, min(NEAR, groups - 1) + 1):
        tell(barrier, distance)

    small = [
        pltpu.make_async_copy(source, target, small_sems.at[i])
        for i, (source, target) in enumerate(
            [
                (decay_hbm, decay_ref),
                (area_hbm, area_ref),
                (bus_hbm, bus_ref),
                (sens_hbm.at[0], sens_ref),
                (counts_hbm, counts_ref),
                (out_map_hbm, out_map_ref),
                (rule_hbm, rule_ref),
                (knots_hbm, knots_ref),
                (levels_hbm, levels_ref),
            ]
        )
    ]
    for copy in small:
        copy.start()

    def load_copies(b):
        own = pl.ds(b * batch, batch)
        return (
            pltpu.make_async_copy(map_hbm.at[own], map_ref.at[own], load_sems.at[0, b]),
            pltpu.make_async_copy(load_hbm.at[own], load_ref.at[own], load_sems.at[1, b]),
        )

    for copy in load_copies(0):
        copy.start()

    def decay_copy(part, step):
        own = pl.ds(part * half, half)
        return pltpu.make_async_remote_copy(
            src_ref=decay_ref.at[:, own],
            dst_ref=later_decay.at[step - 1, :, own],
            send_sem=decay_sems.at[0, part, step - 1],
            recv_sem=decay_sems.at[1, part, step - 1],
            device_id=(group, turn - step),
            device_id_type=MESH,
        )

    with jax.named_scope("prep_ranks"):
        small[1].wait()
        small[2].wait()
        for b in range(1, BATCHES):
            for copy in load_copies(b):
                copy.start()
        ids_row = lax.broadcasted_iota(jnp.int32, (feeders, feeders), 1)
        ids_col = lax.broadcasted_iota(jnp.int32, (feeders, feeders), 0)
        area_row = area_ref[...].astype(jnp.float32)
        area_col = jnp.concatenate([area_row] * 8, axis=0).T[:, :1]
        peers = (area_col == area_row) & (ids_col // per_dev == ids_row // per_dev)
        rank_row = jnp.sum(jnp.where(peers & (ids_col < ids_row), 1.0, 0.0), axis=0, keepdims=True)
        rank_ref[...] = jnp.concatenate([area_row] * 4 + [rank_row] * 4, axis=0).T

        place = lax.broadcasted_iota(jnp.int32, (groups * SLOT_ROWS, feeders), 0)
        owner = lax.broadcasted_iota(jnp.int32, (groups * SLOT_ROWS, feeders), 1) // per_dev
        slot = lax.rem(place, SLOT_ROWS)
        wanted = (place // SLOT_ROWS == owner) & (area_ref[...] == group) & (slot < 2 * CAP)
        chosen = one_hot(wanted & (rank_row == lax.rem(slot, CAP).astype(jnp.float32)))
        bus_ids = lax.broadcasted_iota(jnp.int32, (buses, feeders), 0)
        owned = (bus_ids == bus_ref[...]) & (area_ref[...] == group)
        hot = one_hot(owned)
        sources = dot_nt(chosen, hot).astype(jnp.bfloat16)

    with jax.named_scope("barrier"):
        near = [tellers(distance) for distance in range(1, min(NEAR, groups - 1) + 1)]
        pl.semaphore_wait(barrier, turns - 1 + sum(near))
    reach = [NEAR << i for i in range(groups) if NEAR << i < groups]
    if reach:
        tell(reach_sems.at[0], reach[0])
    small[0].wait()
    for part in range(2):
        for step in range(turns - 1, 0, -1):

            @pl.when(turn >= step)
            def _():
                decay_copy(part, step).start()

    with jax.named_scope("prep_pairs"):
        small[3].wait()
        picked = [sum(dot_nt(sources, term) for term in split(sens_ref[k])) for k in range(2)]
        kind = lax.broadcasted_iota(jnp.int32, (groups * SLOT_ROWS, buses), 0)
        kind = lax.rem(kind, SLOT_ROWS) // CAP
        picked = jnp.where(kind == 0, picked[0], picked[1])
        pairs = sum(dot(term, hot) for term in split(picked))
        pair_send[...] = pairs.reshape(groups, SLOT_ROWS, feeders)

    def pair_copy(step):
        target = lax.rem(group + step, groups)
        return pltpu.make_async_remote_copy(
            src_ref=pair_send.at[target],
            dst_ref=pair_recv.at[step],
            send_sem=pair_sems.at[0, step - 1],
            recv_sem=pair_sems.at[1, step - 1],
            device_id=(target, turn),
            device_id_type=MESH,
        )

    with jax.named_scope("prep_maps"):
        small[4].wait()
        small[5].wait()
        same = lax.broadcasted_iota(jnp.int32, (per_dev, per_dev), 0) == lax.broadcasted_iota(
            jnp.int32, (per_dev, per_dev), 1
        )
        limit = jnp.sum(
            jnp.where(same, counts_ref[...].astype(jnp.float32), 0.0), axis=1, keepdims=True
        )
        state_ids = lax.broadcasted_iota(jnp.int32, (per_dev, width), 1).astype(jnp.float32)
        maps = [jnp.where(state_ids < limit, out_map_ref[:, k, :], 0.0) for k in range(2)]

    with jax.named_scope("columns"):
        parts = [split(m) for m in maps]
        columns = [p[0] for p in parts] + [p[1] for p in parts]
        blank = jnp.zeros((128 - 4 * per_dev, width), jnp.float32)
        columns = [c.astype(jnp.float32) for c in columns] + [blank]
        columns = jnp.concatenate(columns, axis=0).T.astype(jnp.bfloat16)
        lane_ids = lax.rem(lax.broadcasted_iota(jnp.int32, (1, 128), 1), per_dev)
        for f in range(per_dev):
            column_ref[f * width : (f + 1) * width] = columns * one_hot(lane_ids == f)

    def states(b):
        for copy in load_copies(b):
            copy.wait()
        for f in range(b * batch, (b + 1) * batch):
            own = slice(f * width, (f + 1) * width)
            state = None
            for part in range(2):
                first = part * couples
                load = load_ref[f, couples:] if part else load_ref[f, :couples]
                drive = dot(load.reshape(load.shape[0] * scen, nodes), map_ref[f])
                for t in range(load.shape[0]):
                    push = drive[t * scen : (t + 1) * scen]
                    row = (first + t) * scen
                    if state is None:
                        state = push
                    else:
                        state = decay_ref[first + t, f : f + 1, :] * state + push
                    upper, lower = split(state)
                    state_ref[row : row + scen, own] = upper
                    state_ref[span * scen + row : span * scen + row + scen, own] = lower

    def local_flow(b):
        own = slice(b * batch * width, (b + 1) * batch * width)
        upper = dot(state_ref[: span * scen, own], column_ref[own])
        value = upper + dot(state_ref[span * scen :, own], column_ref[own])
        local_ref[...] = local_ref[...] + value if b else value

    def pass_on(i):
        with jax.named_scope("reach%d" % i):
            pl.semaphore_wait(reach_sems.at[i], tellers(reach[i]))
        if i + 1 < len(reach):
            tell(reach_sems.at[i + 1], reach[i + 1])

    last = BATCHES - 2
    rounds = [max(0, last - (len(reach) - 1 - i)) if i else 0 for i in range(len(reach))]
    for b in range(BATCHES):
        with jax.named_scope("states%d" % b):
            states(b)
            if b:
                local_flow(b - 1)
        for i, place in enumerate(rounds):
            if place == b:
                pass_on(i)
        if b == last:
            for step in range(1, groups):
                pair_copy(step).start()

    def put_rows(row, value):
        for lane in range(width // 128):
            weight_ref[lane, pl.ds(row, half, stride=rows), :] = value[
                :, lane * 128 : (lane + 1) * 128
            ]

    def products(part):
        own = slice(part * half, (part + 1) * half)
        product = jnp.ones((half, width), jnp.float32)
        for step in range(turns - 1):
            for t in range(span):
                product = product * later_decay[step, t, own]
                for k in range(2):
                    row = (t % 2) * later_rows + (step * couples + t // 2) * 2 + k
                    put_rows(part * half * rows + row, maps[k][own] * product)

    end = [slice((n * span - 1) * scen, n * span * scen) for n in (1, 2)]

    def later_flow(part):
        for index in range(half):
            f = part * half + index
            weight = jnp.concatenate(
                [weight_ref[lane, f * rows : (f + 1) * rows, :] for lane in range(width // 128)],
                axis=1,
            )
            stacked = jnp.concatenate(split(weight), axis=0)
            own = slice(f * width, (f + 1) * width)
            later = dot_nt(stacked, state_ref[end[0], own]) + dot_nt(stacked, state_ref[end[1], own])
            later = later[:rows] + later[rows:]
            flow_send[part, pl.ds(index, later_rows, stride=half), :] = jnp.concatenate(
                [later[:later_rows], later[later_rows:]], axis=1
            )

    def flow_copy(part, step):
        return pltpu.make_async_remote_copy(
            src_ref=flow_send.at[part, pl.ds((step - 1) * piece, piece)],
            dst_ref=flow_recv.at[part, step - 1],
            send_sem=flow_sems.at[0, part, step - 1],
            recv_sem=flow_sems.at[1, part, step - 1],
            device_id=(group, turn + step),
            device_id_type=MESH,
        )

    def send_flow(part):
        for step in range(1, turns):

            @pl.when(turn + step < turns)
            def _():
                flow_copy(part, step).start()

    for part in range(2):
        with jax.named_scope("decaywait%d" % part):
            for step in range(1, turns):

                @pl.when(turn >= step)
                def _():
                    decay_copy(part, step).wait_send()

                @pl.when(turn + step < turns)
                def _():
                    decay_copy(part, step).wait_recv()

        if turns > 1:
            with jax.named_scope("later%d" % part):
                products(part)
                later_flow(part)
        send_flow(part)

    with jax.named_scope("local_last"):
        local_flow(BATCHES - 1)
        local = local_ref[...].T
        local = local[: 2 * per_dev] + local[2 * per_dev : 4 * per_dev]

    with jax.named_scope("effect"):
        pair_recv[0] = pair_send[group]
        for step in range(1, groups):
            pair_copy(step).wait()
        places = groups * SLOT_ROWS
        mine = rank_ref[pl.ds(pl.multiple_of(group * per_dev, 8), per_dev), :]
        mine = jnp.concatenate([mine, mine], axis=0)
        place = lax.broadcasted_iota(jnp.int32, (2 * per_dev, places), 1)
        kind = lax.broadcasted_iota(jnp.int32, (2 * per_dev, places), 0) // per_dev
        source = lax.rem(group + groups - place // SLOT_ROWS, groups).astype(jnp.float32)
        slot = lax.rem(place, SLOT_ROWS)
        taken = (mine[:, :1] == source) & (slot // CAP == kind)
        taken = one_hot(taken & (mine[:, 4:5] == lax.rem(slot, CAP).astype(jnp.float32)))
        upper, lower = [
            dot(taken, term).T.astype(jnp.bfloat16)
            for term in split(pair_recv[...].reshape(places, feeders))
        ]
        effect = jnp.concatenate([upper, upper, lower], axis=1)

    with jax.named_scope("flowwait"):
        for part in range(2):
            for step in range(1, turns):

                @pl.when(turn >= step)
                def _():
                    flow_copy(part, step).wait_recv()

                @pl.when(turn < step)
                def _():
                    flow_recv[part, step - 1] = jnp.zeros((piece, 2 * scen), jnp.float32)

    def other(k):
        return k + lax.div(groups + k - group, groups)

    def volt_copy(k):
        return pltpu.make_async_remote_copy(
            src_ref=volt_send.at[other(k)],
            dst_ref=volt_recv.at[group],
            send_sem=volt_sems.at[0, k],
            recv_sem=volt_sems.at[1, group],
            device_id=(other(k), turn),
            device_id_type=MESH,
        )

    def volt_arrival(k):
        return pltpu.make_async_remote_copy(
            src_ref=volt_send.at[other(k)],
            dst_ref=volt_recv.at[other(k)],
            send_sem=volt_sems.at[0, k],
            recv_sem=volt_sems.at[1, other(k)],
            device_id=(other(k), turn),
            device_id_type=MESH,
        )

    with jax.named_scope("shift"):
        arrived = [
            sum(flow_recv[part, step] for step in range(turns - 1))
            if turns > 1
            else jnp.zeros((piece, 2 * scen), jnp.float32)
            for part in range(2)
        ]
        for couple in range(couples):
            extra = [
                arrived[part][(couple * 2 + k) * half : (couple * 2 + k + 1) * half]
                for k in range(2)
                for part in range(2)
            ]
            sources = local[:, couple * 2 * scen : (couple + 1) * 2 * scen]
            upper, lower = split(sources + jnp.concatenate(extra, axis=0))
            sources = jnp.concatenate([upper, lower, upper], axis=0)
            volt_send[:, couple] = dot(effect, sources).reshape(groups, per_dev, 2 * scen)

    for k in range(groups - 1):
        volt_copy(k).start()

    with jax.named_scope("rules"):
        for copy in small[6:]:
            copy.wait()
        rules = knots_ref.shape[1]
        rule_ids = lax.broadcasted_iota(jnp.int32, (rules, feeders), 0)
        rule_hot = jnp.where(rule_ids == rule_ref[...], 1.0, 0.0)
        table = jnp.concatenate(
            [knots_ref[...].astype(jnp.float32), levels_ref[...].astype(jnp.float32)], axis=0
        )
        chosen = jnp.dot(table, rule_hot, precision=HIGH, preferred_element_type=jnp.float32)
        rule_vals[...] = (chosen / 1000.0).T

    mine = rule_vals[pl.ds(pl.multiple_of(group * per_dev, 8), per_dev), :]
    knot_count = knots_ref.shape[0]
    knots = [mine[:, i : i + 1] for i in range(knot_count)]
    levels = [mine[:, knot_count + i : knot_count + i + 1] for i in range(knot_count)]
    spans = [knots[i + 1] - knots[i] for i in range(knot_count - 1)]
    slopes = [(levels[i + 1] - levels[i]) / spans[i] for i in range(knot_count - 1)]
    with jax.named_scope("voltwait"):
        volts = volt_send[group]
        for k in range(groups - 1):
            volt_arrival(k).wait_recv()
            volts = volts + volt_recv[other(k)]
    with jax.named_scope("rule"):
        for couple in range(couples):
            value = volts[couple]
            result = levels[0] + jnp.zeros_like(value)
            for i in range(knot_count - 1):
                inside = jnp.minimum(jnp.maximum(value - knots[i], 0.0), spans[i])
                result = result + slopes[i] * inside
            out_ref[2 * couple] = result[:, :scen]
            out_ref[2 * couple + 1] = result[:, scen:]

    for k in range(groups - 1):
        volt_copy(k).wait_send()
    for part in range(2):
        for step in range(1, turns):

            @pl.when(turn + step < turns)
            def _():
                flow_copy(part, step).wait_send()


def per_device(
    node_load,
    drive_map,
    decay_rate,
    counts,
    out_map,
    area_of,
    head_bus,
    rule_of,
    rule_knots,
    levels,
    sensitivity,
):
    groups, turns = lax.axis_size("feeder"), lax.axis_size("tm")
    per_dev, scen, span, nodes = node_load.shape
    width = drive_map.shape[2]
    feeders = head_bus.shape[0]
    buses = sensitivity.shape[2]
    half, couples = per_dev // 2, span // 2
    later_rows = -(-(turns - 1) * span // 8) * 8
    rows = max(2 * later_rows, 8)
    piece = couples * 2 * half
    vmem = pl.BlockSpec(memory_space=pltpu.VMEM)
    hbm = pl.BlockSpec(memory_space=pltpu.HBM)
    f32, i32 = jnp.float32, jnp.int32
    dma = pltpu.SemaphoreType.DMA
    operands = (
        jnp.transpose(node_load, (0, 2, 1, 3)),
        drive_map,
        jnp.transpose(decay_rate, (1, 0, 2)),
        counts.reshape(1, per_dev),
        out_map,
        area_of.reshape(1, feeders),
        head_bus.reshape(1, feeders),
        rule_of.reshape(1, feeders),
        rule_knots.T,
        levels.T,
        sensitivity,
    )
    settings = pl.pallas_call(
        functools.partial(kernel, groups, turns),
        out_shape=jax.ShapeDtypeStruct((span, per_dev, scen), f32),
        in_specs=[hbm] * len(operands),
        out_specs=vmem,
        scratch_shapes=[
            pltpu.VMEM((per_dev, span, scen, nodes), node_load.dtype),
            pltpu.VMEM((per_dev, nodes, width), drive_map.dtype),
            pltpu.VMEM((2, buses, buses), f32),
            pltpu.VMEM((span, per_dev, width), f32),
            pltpu.VMEM((1, per_dev), i32),
            pltpu.VMEM(out_map.shape, f32),
            pltpu.VMEM((1, feeders), i32),
            pltpu.VMEM((1, feeders), i32),
            pltpu.VMEM((1, feeders), i32),
            pltpu.VMEM(rule_knots.shape[::-1], i32),
            pltpu.VMEM(levels.shape[::-1], i32),
            pltpu.VMEM((turns - 1, span, per_dev, width), f32),
            pltpu.VMEM((groups, SLOT_ROWS, feeders), f32),
            pltpu.VMEM((groups, SLOT_ROWS, feeders), f32),
            pltpu.VMEM((width // 128, per_dev * rows, 128), f32),
            pltpu.VMEM((2 * span * scen, per_dev * width), jnp.bfloat16),
            pltpu.VMEM((per_dev * width, 128), jnp.bfloat16),
            pltpu.VMEM((span * scen, 128), f32),
            pltpu.VMEM((feeders, 8), f32),
            pltpu.VMEM((feeders, 2 * rule_knots.shape[1]), f32),
            pltpu.VMEM((2, later_rows * half, 2 * scen), f32),
            pltpu.VMEM((2, turns - 1, piece, 2 * scen), f32),
            pltpu.VMEM((groups, couples, per_dev, 2 * scen), f32),
            pltpu.VMEM((groups, couples, per_dev, 2 * scen), f32),
            dma((2, BATCHES)),
            dma((9,)),
            pltpu.SemaphoreType.REGULAR((8,)),
            dma((2, 2, turns - 1)),
            dma((2, groups - 1)),
            dma((2, 2, turns - 1)),
            dma((2, groups)),
        ],
        compiler_params=pltpu.CompilerParams(
            collective_id=0, has_side_effects=True, vmem_limit_bytes=VMEM_LIMIT
        ),
    )(*[pltpu.with_memory_space_constraint(x, pltpu.HBM) for x in operands])
    return jnp.transpose(settings, (1, 0, 2))


VMEM_LIMIT = 48 * 2**20


def solution(mesh):
    return jax.shard_map(
        per_device,
        mesh=mesh,
        in_specs=(
            P("feeder", None, "tm", None),
            P("feeder", None, None),
            P("feeder", "tm", None),
            P("feeder"),
            P("feeder", None, None),
            P(),
            P(),
            P(),
            P(),
            P(),
            P("feeder", None, None, None),
        ),
        out_specs=P("feeder", "tm", None),
        check_vma=False,
    )
```
